512 devices in a mesh: row: 16 (over z), col: 32 (over y, x, core).
Axes of the slice: x: 4, y: 4, z: 16, core: 2. Of those that a mesh axis runs over, the one named last changes fastest.
Arguments:
- right_side: bfloat16 [16384, 16384], P('row', 'col'), may hold values from -180 to 180
- theta_left: bfloat16 [512, 16384], P(None, 'row'), may hold values from -0.125 to 0.125
- theta_right: bfloat16 [512, 16384], P(None, 'col'), may hold values from -0.125 to 0.125
- query_rows: int32 [1024, 2], replicated, may hold values from 0 to 16384, as said below
- query_cols: int32 [1024, 2], replicated, may hold values from 0 to 16384, as said below
Outputs:
- residual: float32 [16384, 16384], P('row', 'col')
- step_ratio: float32 [1], replicated
- answers: float32 [1024], replicated
The draws below stay inside these ranges and needn't reach their ends.
Inputs may be any that keep to these rules, and one draw needn't show every extreme that they name: `query_rows`: each row is a start and an end with 0 <= start < end <= 16384. `query_cols`: each row is a start and an end with 0 <= start < end <= 16384.
All inputs are finite; a program needn't handle non-finite values.
Results may differ from the reference program's by a relative error of at most 0.0003.
Values sent between devices are 32-bit elements; how exact they have to be, the bound alone decides.
A program may use at most 64 MiB of HBM per device.

```python
import jax
import jax.numpy as jnp
from jax import lax

NR = 16384
NC = 16384
P_SIZE = 512
NQ = 1024


def draw_right_side(key, part):
    noise_key, row_key, col_key = jax.random.split(key, 3)
    base_values = jnp.clip(jax.random.normal(noise_key, (NR, NC), jnp.float32), -6.0, 6.0)
    rise_factor = 3.0
    row_scale = jnp.exp(jax.random.uniform(row_key, (NR, 1), jnp.float32, -1.15, 1.15))
    col_scale = jnp.exp(jax.random.uniform(col_key, (1, NC), jnp.float32, -1.15, 1.15))
    row_trend = rise_factor ** (jnp.arange(NR, dtype=jnp.float32) / NR - 0.5)
    col_trend = 3.0 ** (jnp.arange(NC, dtype=jnp.float32) / NC - 0.5)
    return (base_values * row_scale * col_scale * row_trend[:, None] * col_trend[None, :]).astype(jnp.bfloat16)


def bounds_pair(key, extent):
    start_key, span_key = jax.random.split(key)
    starts = jax.random.randint(start_key, (NQ,), 0, extent)
    span_lengths = 1 + jax.random.randint(span_key, (NQ,), 0, extent) % (extent - starts)
    ends = (starts + span_lengths).at[0].set(extent)
    starts = starts.at[0].set(0)
    return jnp.stack([starts, ends], axis=1).astype(jnp.int32)


def draw_query_rows(key, part):
    return bounds_pair(jax.random.fold_in(key, 11), NR)


def draw_query_cols(key, part):
    return bounds_pair(jax.random.fold_in(key, 23), NC)


def level_of(stream_key, dims, cuts, smallest, top_value):
    gain = 1.0
    for axis_at, blocks in cuts:
        heights = jax.random.uniform(jax.random.fold_in(jax.random.fold_in(stream_key, 6), axis_at), (blocks,), jnp.float32, smallest / len(cuts), top_value / len(cuts))
        gain = gain * jnp.repeat(jnp.exp(heights), dims[axis_at] // blocks).reshape((-1,) + (1,) * (len(dims) - 1 - axis_at))
    return gain


def gaussian(rng, shape, width, reach, shards=(), kind=jnp.bfloat16):
    drawn = width * jax.random.normal(rng, shape, jnp.float32)
    if shards:
        drawn = drawn * level_of(rng, shape, shards, -0.22, 0.18)
    return jnp.clip(drawn, -reach, reach).astype(kind)


def setup_inputs(seed: int = 0) -> dict:
    key_of = jax.random.split(jax.random.key(seed), 6)
    return {
        "right_side": draw_right_side(jax.random.fold_in(key_of[5], 71), 0),
        "theta_left": gaussian(key_of[1], (P_SIZE, NR), (NR // 8) ** -0.5, 0.125, ((1, 16),)),
        "theta_right": gaussian(key_of[2], (P_SIZE, NC), (NC // 8) ** -0.5, 0.125, ((1, 32),)),
        "query_rows": draw_query_rows(jax.random.fold_in(key_of[5], 71), 0),
        "query_cols": draw_query_cols(jax.random.fold_in(key_of[5], 71), 0),
    }


def reference(right_side, theta_left, theta_right, query_rows, query_cols):
    highest = lax.Precision.HIGHEST
    start_field = right_side.astype(jnp.float32)
    left_wide = theta_left.astype(jnp.float32)
    right_wide = theta_right.astype(jnp.float32)
    summed_right = lax.dot_general(right_side, theta_right, (((1,), (1,)), ((), ())), preferred_element_type=jnp.float32)
    middle = start_field + jnp.dot(summed_right, right_wide, precision=highest, preferred_element_type=jnp.float32)
    summed_left = jnp.dot(left_wide, middle, precision=highest, preferred_element_type=jnp.float32)
    image_field = middle + lax.dot_general(left_wide, summed_left, (((0,), (0,)), ((), ())), precision=highest, preferred_element_type=jnp.float32)
    start_norm = jnp.sum(start_field * start_field)
    curvature = jnp.sum(start_field * image_field)
    alpha_step = start_norm / curvature
    residual = start_field - alpha_step * image_field
    step_ratio = (jnp.sum(residual * residual) / start_norm).reshape(1)
    solution = alpha_step * start_field
    prefix = jnp.cumsum(jnp.cumsum(solution, axis=1), axis=0)
    padded = jnp.pad(prefix, ((1, 0), (1, 0)))
    low_row = query_rows[:, 0]
    high_row = query_rows[:, 1]
    low_col = query_cols[:, 0]
    high_col = query_cols[:, 1]
    combined = padded[high_row, high_col] - padded[low_row, high_col] - padded[high_row, low_col] + padded[low_row, low_col]
    area = (high_row - low_row).astype(jnp.float32) * (high_col - low_col).astype(jnp.float32)
    answers = combined / jnp.sqrt(area)
    return (residual, step_ratio, answers)
```

```python
import functools

import jax
import jax.numpy as jnp
from jax import lax
from jax.experimental import pallas as pl
from jax.experimental.pallas import tpu as pltpu
from jax.sharding import PartitionSpec as P

MESH = pl.DeviceIdType.MESH
F32, BF16 = jnp.float32, jnp.bfloat16
NZ, NX, NY = 16, 4, 4
ROWS, COLS, Q, NQ = 1024, 512, 512, 1024
NSUB = 2
SUBW = COLS // NSUB
MSG = NQ + 256
NT = (((1,), (1,)), ((), ()))


def dot(a, b):
    return jnp.dot(a, b, preferred_element_type=F32)


def split(value):
    high = value.astype(BF16)
    return high, (value - high.astype(F32)).astype(BF16)


def dot_split(value, b):
    high, low = split(value)
    return dot(high, b) + dot(low, b)


def copy_to(src, dst, send, recv, device):
    return pltpu.make_async_remote_copy(
        src_ref=src, dst_ref=dst, send_sem=send, recv_sem=recv, device_id=device, device_id_type=MESH
    )


def kernel(
    v_ref, l_ref, r_ref, qr_ref, qc_ref,
    out_ref, ans_ref, ratio_ref,
    lt, bt, sp, sp_in, rs_in, s_full, tp, t_right, t_left, t_full, u_out, u_in, u_all, u_tile, u_full,
    x1, resid, z_hi, z_lo, m_own, m_z, m_plane, m_pair, e_own, e_z, e_plane, e_pair,
    pair_s, pair_r, one_s, one_r, fwd_s, fwd_r, tr_s, tr_r, tl_s, tl_r, gr_s, gr_r, gl_s, gl_r, out_sem,
):
    z = lax.axis_index("row")
    c = lax.axis_index("col")
    core = lax.rem(c, 2)
    chip = c // 2
    xx = lax.rem(chip, NX)
    yy = chip // NX

    def z_peer(d):
        return (lax.rem(z + d, NZ), c)

    def plane_chip(j):
        return lax.rem(yy + j // NX, NY) * NX + lax.rem(xx + lax.rem(j, NX), NX)

    def plane_peer(j):
        return (z, plane_chip(j) * 2 + core)

    other = (z, chip * 2 + 1 - core)
    right, left = z_peer(1), z_peer(NZ - 1)

    barrier = pltpu.get_barrier_semaphore()

    def greet(d, carry):
        pl.semaphore_signal(barrier, inc=1, device_id=z_peer(d), device_id_type=MESH)
        pl.semaphore_signal(barrier, inc=1, device_id=plane_peer(d), device_id_type=MESH)
        return carry

    pl.semaphore_signal(barrier, inc=1, device_id=other, device_id_type=MESH)
    lax.fori_loop(1, NZ, greet, 0)

    def s_half(half):
        def tile(i, carry):
            at = pl.multiple_of(half * 256 + i * 128, 128)
            sp[pl.ds(at, 128), :] = lax.dot_general(
                r_ref[pl.ds(at, 128), :], v_ref[...], NT, preferred_element_type=F32
            )
            return carry

        lax.fori_loop(0, 2, tile, 0)

    def t_tile(i, carry):
        at = pl.multiple_of(i * 128, 128)
        tp[pl.ds(at, 128), :] = dot(l_ref[pl.ds(at, 128), :], v_ref[...])
        return carry

    s_half(1 - core)
    lax.fori_loop(0, 4, t_tile, 0)
    pl.semaphore_wait(barrier, 31)

    give = (1 - core) * 256
    keep = core * 256

    def chunk_rows(base, d):
        return pl.ds(pl.multiple_of(base + lax.rem(yy + d, NY) * 64, 64), 64)

    def pair_copy(d):
        return copy_to(
            sp.at[chunk_rows(give, d)], sp_in.at[chunk_rows(0, d)], pair_s.at[d], pair_r.at[d], other
        )

    for d in (1, 2, 3, 0):
        pair_copy(d).start()

    def t_rows(block):
        return pl.ds(pl.multiple_of(lax.rem(block + 2 * NZ, NZ) * 32, 32), 32)

    def sub(h):
        return pl.ds(h * SUBW, SUBW)

    def t_rs(s):
        for h in range(NSUB):
            if s <= 7:
                rows = t_rows(z + 8 - s)
                if s == 1:
                    src = tp.at[rows, sub(h)]
                else:
                    src = t_right.at[s - 2, :, sub(h)]
                    copy_to(src, src, tr_s.at[s - 2, h], tr_r.at[s - 2, h], right).wait_recv()
                    t_right[s - 2, :, sub(h)] = t_right[s - 2, :, sub(h)] + tp[rows, sub(h)]
                copy_to(src, t_right.at[s - 1, :, sub(h)], tr_s.at[s - 1, h], tr_r.at[s - 1, h], right).start()
            rows = t_rows(z - 9 + s)
            if s == 1:
                src = tp.at[rows, sub(h)]
            else:
                src = t_left.at[s - 2, :, sub(h)]
                copy_to(src, src, tl_s.at[s - 2, h], tl_r.at[s - 2, h], left).wait_recv()
                t_left[s - 2, :, sub(h)] = t_left[s - 2, :, sub(h)] + tp[rows, sub(h)]
            copy_to(src, t_left.at[s - 1, :, sub(h)], tl_s.at[s - 1, h], tl_r.at[s - 1, h], left).start()

    def t_own():
        rows = t_rows(z)
        total = jnp.zeros((1, SUBW), F32)
        for h in range(NSUB):
            a, b = t_right.at[6, :, sub(h)], t_left.at[7, :, sub(h)]
            copy_to(a, a, tr_s.at[6, h], tr_r.at[6, h], right).wait_recv()
            copy_to(b, b, tl_s.at[7, h], tl_r.at[7, h], left).wait_recv()
            block = tp[rows, sub(h)] + t_right[6, :, sub(h)] + t_left[7, :, sub(h)]
            t_full[rows, sub(h)] = block
            total = total + jnp.sum(block * block, axis=0, keepdims=True)
        return jnp.sum(total)

    def t_ag(s):
        for h in range(NSUB):
            if s <= 8:
                if s <= 7:
                    here = t_full.at[t_rows(z - s + 1), sub(h)]
                    if s > 1:
                        copy_to(here, here, gr_s.at[s - 2, h], gr_r.at[s - 2, h], right).wait_recv()
                    copy_to(here, here, gr_s.at[s - 1, h], gr_r.at[s - 1, h], right).start()
                here = t_full.at[t_rows(z + s - 1), sub(h)]
                if s > 1:
                    copy_to(here, here, gl_s.at[s - 2, h], gl_r.at[s - 2, h], left).wait_recv()
                copy_to(here, here, gl_s.at[s - 1, h], gl_r.at[s - 1, h], left).start()
            else:
                here = t_full.at[t_rows(z - 7), sub(h)]
                copy_to(here, here, gr_s.at[6, h], gr_r.at[6, h], right).wait_recv()
                here = t_full.at[t_rows(z + 8), sub(h)]
                copy_to(here, here, gl_s.at[7, h], gl_r.at[7, h], left).wait_recv()

    t_rs(1)
    s_half(core)

    def plane_copy(j):
        rows = pl.ds(pl.multiple_of(keep + plane_chip(j) * 16, 16), 16)
        return copy_to(sp.at[rows], rs_in.at[j - 1], one_s.at[0], one_r.at[0], plane_peer(j))

    for d in (1, 2, 3, 0):
        pair_copy(d).wait_recv()
        mine, got = chunk_rows(keep, d), chunk_rows(0, d)
        sp[mine, :] = sp[mine, :] + sp_in[got, :]

        def send(j, carry):
            plane_copy(j).start()
            return carry

        lax.fori_loop(4 * d if d else 1, 4 * d + 4, send, 0)

    t_rs(2)

    def lt_tile(i, carry):
        at = pl.multiple_of(i * 128, 128)
        lt[pl.ds(at, 128), :] = l_ref[:, pl.ds(at, 128)].astype(F32).T.astype(BF16)
        return carry

    lax.fori_loop(0, 4, lt_tile, 0)
    t_rs(3)
    lax.fori_loop(4, 8, lt_tile, 0)

    def bt_tile(i, carry):
        at = pl.multiple_of(i * 128, 128)
        index = lax.broadcasted_iota(jnp.int32, (128, NQ), 0) + (at + c * COLS)
        inside = (index >= qc_ref[0:1, :]) & (index < qc_ref[1:2, :])
        bt[pl.ds(at, 128), :] = jnp.where(inside, 1.0, 0.0).astype(BF16)
        return carry

    lax.fori_loop(0, 4, bt_tile, 0)
    t_rs(4)

    def answer_tile(i, carry):
        total, norm = carry
        at = pl.multiple_of(i * 128, 128)
        block = v_ref[pl.ds(at, 128), :]
        across = dot(block, bt[...])
        index = lax.broadcasted_iota(jnp.int32, (128, NQ), 0) + (at + z * ROWS)
        inside = (index >= qr_ref[0:1, :]) & (index < qr_ref[1:2, :])
        total = total + jnp.sum(jnp.where(inside, across, 0.0), axis=0, keepdims=True)
        wide = block.astype(F32)
        norm = norm + jnp.sum(wide * wide, axis=0, keepdims=True)
        return total, norm

    carry = (jnp.zeros((1, NQ), F32), jnp.zeros((1, COLS), F32))
    carry = lax.fori_loop(0, 3, answer_tile, carry)
    t_rs(5)
    carry = lax.fori_loop(3, 6, answer_tile, carry)
    t_rs(6)
    carry = lax.fori_loop(6, 8, answer_tile, carry)
    m_own[:, 0:NQ] = carry[0]
    m_own[:, NQ : NQ + 128] = jnp.broadcast_to(jnp.sum(carry[1]), (1, 128))

    copy_to(rs_in, rs_in, one_s.at[0], one_r.at[0], other).wait_recv()
    own_rows = pl.ds(pl.multiple_of(keep + chip * 16, 16), 16)

    def add_in(j, total):
        return total + rs_in[j]

    s_block = lax.fori_loop(0, 15, add_in, sp[own_rows, :])
    s_full[own_rows, :] = s_block

    def s_copy(j):
        here = s_full.at[own_rows]
        return copy_to(here, here, one_s.at[1], one_r.at[1], plane_peer(j))

    def start_all(make):
        def one(j, carry):
            make(j).start()
            return carry

        lax.fori_loop(1, 16, one, 0)

    s_high, s_low = split(s_block)
    u_part = lax.dot_general(s_high, l_ref[...], NT, preferred_element_type=F32) + lax.dot_general(
        s_low, l_ref[...], NT, preferred_element_type=F32
    )
    for i in range(NZ):
        u_out[i] = u_part[i : i + 1, :]

    def u_copy(d):
        return copy_to(u_out.at[lax.rem(z + d, NZ)], u_in.at[d - 1], one_s.at[2], one_r.at[2], z_peer(d))

    start_all(u_copy)
    start_all(s_copy)
    rest = jnp.sum(s_block * s_block)
    t_rs(7)
    t_rs(8)
    rest = rest + t_own()
    t_ag(1)

    copy_to(u_in, u_in, one_s.at[2], one_r.at[2], other).wait_recv()

    def add_row(j, total):
        return total + u_in[j]

    u_row = lax.fori_loop(0, 15, add_row, u_out[z])
    u_all[z] = u_row

    def ug_copy(d):
        return copy_to(u_all.at[z], u_all.at[z], one_s.at[3], one_r.at[3], z_peer(d))

    start_all(ug_copy)
    rest = rest + jnp.sum(u_row * u_row)
    m_own[:, NQ + 128 :] = jnp.broadcast_to(rest, (1, 128))

    def m_copy(d):
        return copy_to(m_own, m_z.at[d - 1], one_s.at[4], one_r.at[4], z_peer(d))

    start_all(m_copy)
    t_ag(2)

    copy_to(s_full.at[0:240], s_full.at[0:240], one_s.at[1], one_r.at[1], other).wait_recv()
    kept = s_full.at[pl.ds(pl.multiple_of(keep, 256), 256)]
    given = s_full.at[pl.ds(pl.multiple_of(give, 256), 256)]
    copy_to(kept, kept, fwd_s.at[0], fwd_r.at[0], other).start()
    t_ag(3)

    copy_to(u_all.at[0:15], u_all.at[0:15], one_s.at[3], one_r.at[3], other).wait_recv()
    for i in range(NZ):
        u_tile[i : i + 1, :] = u_all[i]
    u_full[own_rows, :] = u_tile[...]

    def up_copy(j):
        here = u_full.at[own_rows]
        return copy_to(here, here, one_s.at[5], one_r.at[5], plane_peer(j))

    start_all(up_copy)

    copy_to(m_z, m_z, one_s.at[4], one_r.at[4], other).wait_recv()

    def add_m(buffer):
        return lambda j, total: total + buffer[j]

    m_plane[15] = lax.fori_loop(0, 15, add_m(m_z), m_own[...])

    def mp_copy(j):
        return copy_to(m_plane.at[15], m_plane.at[j - 1], one_s.at[6], one_r.at[6], plane_peer(j))

    start_all(mp_copy)
    t_ag(4)

    copy_to(given, given, fwd_s.at[0], fwd_r.at[0], other).wait_recv()

    def x_tile(i, carry):
        at = pl.multiple_of(i * 128, 128)
        high, low = split(s_full[:, pl.ds(at, 128)].T)
        x1[pl.ds(at, 128), :] = v_ref[pl.ds(at, 128), :].astype(F32) + dot(high, r_ref[...]) + dot(low, r_ref[...])
        return carry

    lax.fori_loop(0, 3, x_tile, 0)
    t_ag(5)
    lax.fori_loop(3, 6, x_tile, 0)
    t_ag(6)
    lax.fori_loop(6, 8, x_tile, 0)

    copy_to(u_full.at[0:240], u_full.at[0:240], one_s.at[5], one_r.at[5], other).wait_recv()
    u_kept = u_full.at[pl.ds(pl.multiple_of(keep, 256), 256)]
    u_given = u_full.at[pl.ds(pl.multiple_of(give, 256), 256)]
    copy_to(u_kept, u_kept, fwd_s.at[1], fwd_r.at[1], other).start()

    copy_to(m_plane.at[0:15], m_plane.at[0:15], one_s.at[6], one_r.at[6], other).wait_recv()
    m_pair[0] = lax.fori_loop(0, 16, add_m(m_plane), jnp.zeros((1, MSG), F32))
    copy_to(m_pair.at[0], m_pair.at[1], fwd_s.at[2], fwd_r.at[2], other).start()
    t_ag(7)
    t_ag(8)

    copy_to(m_pair.at[1], m_pair.at[1], fwd_s.at[2], fwd_r.at[2], other).wait_recv()
    message = m_pair[0] + m_pair[1]
    norm = message[:, NQ : NQ + 128]
    alpha = norm / (norm + message[:, NQ + 128 :])
    spans = (qr_ref[1:2, :] - qr_ref[0:1, :]).astype(F32) * (qc_ref[1:2, :] - qc_ref[0:1, :]).astype(F32)
    alpha = alpha[0:1, 0:1]
    ans_ref[...] = message[:, 0:NQ] * alpha / jnp.sqrt(spans)

    copy_to(u_given, u_given, fwd_s.at[1], fwd_r.at[1], other).wait_recv()
    t_ag(9)

    def z_tile(i, carry):
        at = pl.multiple_of(i * 128, 128)
        high, low = split(u_full[:, pl.ds(at, 128)].T)
        block = t_full[pl.ds(at, 128), :] + dot(high, r_ref[...]) + dot(low, r_ref[...])
        high, low = split(block)
        z_hi[pl.ds(at, 128), :] = high
        z_lo[pl.ds(at, 128), :] = low
        return carry

    lax.fori_loop(0, 4, z_tile, 0)

    def final_tile(i, total):
        at = pl.multiple_of(i * 128, 128)
        rows = lt[pl.ds(at, 128), :]
        image = x1[pl.ds(at, 128), :] + dot(rows, z_hi[...]) + dot(rows, z_lo[...])
        block = v_ref[pl.ds(at, 128), :].astype(F32) - alpha * image
        resid[pl.ds(at, 128), :] = block
        return total + jnp.sum(block * block, axis=0, keepdims=True)

    fresh = lax.fori_loop(0, 8, final_tile, jnp.zeros((1, COLS), F32))
    out_copy = pltpu.make_async_copy(resid, out_ref, out_sem)
    out_copy.start()

    e_own[...] = jnp.broadcast_to(jnp.sum(fresh), (1, 128))

    def ez_copy(d):
        return copy_to(e_own, e_z.at[d - 1], one_s.at[7], one_r.at[7], z_peer(d))

    start_all(ez_copy)
    copy_to(e_z, e_z, one_s.at[7], one_r.at[7], other).wait_recv()
    e_plane[15] = lax.fori_loop(0, 15, add_m(e_z), e_own[...])

    def ep_copy(j):
        return copy_to(e_plane.at[15], e_plane.at[j - 1], one_s.at[8], one_r.at[8], plane_peer(j))

    start_all(ep_copy)
    copy_to(e_plane.at[0:15], e_plane.at[0:15], one_s.at[8], one_r.at[8], other).wait_recv()
    e_pair[0] = lax.fori_loop(0, 16, add_m(e_plane), jnp.zeros((1, 128), F32))
    copy_to(e_pair.at[0], e_pair.at[1], fwd_s.at[3], fwd_r.at[3], other).start()
    copy_to(e_pair.at[1], e_pair.at[1], fwd_s.at[3], fwd_r.at[3], other).wait_recv()
    ratio_ref[...] = (e_pair[0] + e_pair[1]) / norm

    def sent(ref, sem):
        copy_to(ref, ref, sem, one_r.at[0], other).wait_send()

    for d in range(4):
        sent(sp_in.at[0:64], pair_s.at[d])
    sent(rs_in, one_s.at[0])
    sent(s_full.at[0:240], one_s.at[1])
    sent(u_in, one_s.at[2])
    sent(u_all.at[0:15], one_s.at[3])
    sent(m_z, one_s.at[4])
    sent(u_full.at[0:240], one_s.at[5])
    sent(m_plane.at[0:15], one_s.at[6])
    sent(e_z, one_s.at[7])
    sent(e_plane.at[0:15], one_s.at[8])
    sent(kept, fwd_s.at[0])
    sent(u_kept, fwd_s.at[1])
    sent(m_pair.at[0], fwd_s.at[2])
    sent(e_pair.at[0], fwd_s.at[3])
    for h in range(NSUB):
        for s in range(7):
            sent(t_right.at[s, :, sub(h)], tr_s.at[s, h])
            sent(t_right.at[s, :, sub(h)], gr_s.at[s, h])
        for s in range(8):
            sent(t_left.at[s, :, sub(h)], tl_s.at[s, h])
            sent(t_left.at[s, :, sub(h)], gl_s.at[s, h])
    out_copy.wait()


def shards(right_side, theta_left, theta_right, query_rows, query_cols):
    vmem = pl.BlockSpec(memory_space=pltpu.VMEM)
    dma = pltpu.SemaphoreType.DMA
    residual, answers, ratio = pl.pallas_call(
        kernel,
        out_shape=(
            jax.ShapeDtypeStruct((ROWS, COLS), F32),
            jax.ShapeDtypeStruct((1, NQ), F32),
            jax.ShapeDtypeStruct((1, 128), F32),
        ),
        in_specs=[vmem] * 5,
        out_specs=(pl.BlockSpec(memory_space=pl.ANY), vmem, vmem),
        scratch_shapes=[
            pltpu.VMEM((ROWS, Q), BF16),
            pltpu.VMEM((COLS, NQ), BF16),
            pltpu.VMEM((Q, ROWS), F32),
            pltpu.VMEM((256, ROWS), F32),
            pltpu.VMEM((15, 16, ROWS), F32),
            pltpu.VMEM((Q, ROWS), F32),
            pltpu.VMEM((Q, COLS), F32),
            pltpu.VMEM((7, 32, COLS), F32),
            pltpu.VMEM((8, 32, COLS), F32),
            pltpu.VMEM((Q, COLS), F32),
            pltpu.VMEM((NZ, 1, Q), F32),
            pltpu.VMEM((15, 1, Q), F32),
            pltpu.VMEM((NZ, 1, Q), F32),
            pltpu.VMEM((NZ, Q), F32),
            pltpu.VMEM((Q, Q), F32),
            pltpu.VMEM((ROWS, COLS), F32),
            pltpu.VMEM((ROWS, COLS), F32),
            pltpu.VMEM((Q, COLS), BF16),
            pltpu.VMEM((Q, COLS), BF16),
            pltpu.VMEM((1, MSG), F32),
            pltpu.VMEM((15, 1, MSG), F32),
            pltpu.VMEM((16, 1, MSG), F32),
            pltpu.VMEM((2, 1, MSG), F32),
            pltpu.VMEM((1, 128), F32),
            pltpu.VMEM((15, 1, 128), F32),
            pltpu.VMEM((16, 1, 128), F32),
            pltpu.VMEM((2, 1, 128), F32),
            dma((4,)), dma((4,)),
            dma((9,)), dma((9,)),
            dma((4,)), dma((4,)),
            dma((7, NSUB)), dma((7, NSUB)),
            dma((8, NSUB)), dma((8, NSUB)),
            dma((7, NSUB)), dma((7, NSUB)),
            dma((8, NSUB)), dma((8, NSUB)),
            dma,
        ],
        compiler_params=pltpu.CompilerParams(
            collective_id=0, has_side_effects=True, vmem_limit_bytes=48 * 1024 * 1024
        ),
        name="step",
    )(right_side, theta_left, theta_right, query_rows.T, query_cols.T)
    return residual, ratio[0, 0:1], answers.reshape(NQ)


def solution(mesh):
    return jax.shard_map(
        shards,
        mesh=mesh,
        in_specs=(P("row", "col"), P(None, "row"), P(None, "col"), P(), P()),
        out_specs=(P("row", "col"), P(), P()),
        check_vma=False,
    )
```

```python
import functools

import jax
import jax.numpy as jnp
from jax import lax
from jax.experimental import pallas as pl
from jax.experimental.pallas import tpu as pltpu
from jax.sharding import PartitionSpec as P

MESH = pl.DeviceIdType.MESH
F32, BF16 = jnp.float32, jnp.bfloat16
NZ, NX, NY = 16, 4, 4
ROWS, COLS, Q, NQ = 1024, 512, 512, 1024
NSUB = 1
JUMP = 5
SUBW = COLS // NSUB
NT = (((1,), (1,)), ((), ()))


def dot(a, b):
    return jnp.dot(a, b, preferred_element_type=F32)


def split(value):
    high = value.astype(BF16)
    return high, (value - high.astype(F32)).astype(BF16)


def dot_split(value, b):
    high, low = split(value)
    return dot(high, b) + dot(low, b)


def copy_to(src, dst, send, recv, device):
    return pltpu.make_async_remote_copy(
        src_ref=src, dst_ref=dst, send_sem=send, recv_sem=recv, device_id=device, device_id_type=MESH
    )


def kernel(
    v_hbm, l_hbm, r_hbm, qr_ref, qc_ref,
    out_ref, ans_ref, ratio_ref,
    v_ref, l_ref, r_ref,
    lt, bt, sp, sp_in, a_in, b_in, a_sum, b_sum, a2_in, b2_in, s_full,
    tp, t_near_r, t_near_l, t_far_r, t_far_l, t_full, u_out, u_in, u_all, u_tile, u_full, ur,
    x1, resid, z_hi, z_lo, m_out, m_z, m_plane, m_pair, e_z, e_plane, e_pair,
    pair_s, pair_r, one_s, one_r, grp_r, fwd_s, fwd_r, tr_s, tr_r, gr_s, gr_r, in_sem, out_sem,
):
    z = lax.axis_index("row")
    c = lax.axis_index("col")
    core = lax.rem(c, 2)
    chip = c // 2
    xx = lax.rem(chip, NX)
    yy = chip // NX

    def z_peer(d):
        return (lax.rem(z + d, NZ), c)

    def plane_chip(j):
        return lax.rem(yy + j // NX, NY) * NX + lax.rem(xx + lax.rem(j, NX), NX)

    def plane_peer(j):
        return (z, plane_chip(j) * 2 + core)

    def x_peer(d):
        return (z, (yy * NX + lax.rem(xx + d, NX)) * 2 + core)

    def y_peer(d):
        return (z, (lax.rem(yy + d, NY) * NX + xx) * 2 + core)

    other = (z, chip * 2 + 1 - core)
    right, left = z_peer(1), z_peer(NZ - 1)

    loads = [
        pltpu.make_async_copy(src, dst, in_sem.at[i])
        for i, (src, dst) in enumerate(((r_hbm, r_ref), (v_hbm, v_ref), (l_hbm, l_ref)))
    ]
    for load in loads:
        load.start()
    barrier = pltpu.get_barrier_semaphore()

    def greet(d, carry):
        pl.semaphore_signal(barrier, inc=1, device_id=z_peer(d), device_id_type=MESH)
        pl.semaphore_signal(barrier, inc=1, device_id=plane_peer(d), device_id_type=MESH)
        return carry

    pl.semaphore_signal(barrier, inc=1, device_id=other, device_id_type=MESH)
    lax.fori_loop(1, NZ, greet, 0)

    def s_half(half):
        rows = pl.ds(pl.multiple_of(half * 256, 256), 256)

        def tile(i, carry):
            at = pl.multiple_of(i * 256, 256)
            block = lax.dot_general(r_ref[rows, :], v_ref[pl.ds(at, 256), :], NT, preferred_element_type=F32)
            sp[half, :, :, :, :, pl.ds(at, 256)] = block.reshape(NY, NX, 2, 8, 256)
            return carry

        lax.fori_loop(0, 4, tile, 0)

    def t_tile(i, carry):
        at = pl.multiple_of(i * 256, 256)
        tp[pl.ds(at, 256), :] = dot(l_ref[pl.ds(at, 256), :], v_ref[...])
        return carry

    loads[0].wait()
    loads[1].wait()
    s_half(1 - core)
    pl.semaphore_wait(barrier, 31)

    give, keep = (1 - core) * 256, core * 256
    order = (2, 1, 3, 0)

    def x_at(d):
        return lax.rem(xx + d, NX)

    def y_at(d):
        return lax.rem(yy + d, NY)

    def pair_a(d):
        return copy_to(
            sp.at[1 - core, :, x_at(d), 0], sp_in.at[:, x_at(d), 0], pair_s.at[0, d], pair_r.at[0, d], other
        )

    def pair_b(d):
        return copy_to(
            sp.at[1 - core, y_at(d), :, 1], sp_in.at[y_at(d), :, 1], pair_s.at[1, d], pair_r.at[1, d], other
        )

    for d in order:
        pair_a(d).start()
        pair_b(d).start()

    def t_rows(block):
        return pl.ds(pl.multiple_of(lax.rem(block + 2 * NZ, NZ) * 32, 32), 32)

    def sub(h):
        return pl.ds(h * SUBW, SUBW)

    rs_flows = (
        (1, tuple(range(7, JUMP - 1, -1)), t_far_r, 2, True),
        (-1, tuple(range(8, JUMP - 1, -1)), t_far_l, 3, True),
        (1, tuple(range(JUMP - 1, 0, -1)), t_near_r, 0, False),
        (-1, tuple(range(JUMP - 1, 0, -1)), t_near_l, 1, False),
    )

    def t_dev(offset):
        return z_peer(offset + NZ)

    def t_rs(s):
        k = s - 1
        for h in range(NSUB):
            for sign, dist, buf, f, far in rs_flows:
                if k >= len(dist):
                    continue
                rows = t_rows(z + sign * dist[k])
                src = tp.at[rows, sub(h)]
                if k:
                    src = buf.at[k - 1, :, sub(h)]
                    copy_to(src, src, tr_s.at[f, k - 1, h], tr_r.at[f, k - 1, h], right).wait_recv()
                    buf[k - 1, :, sub(h)] = buf[k - 1, :, sub(h)] + tp[rows, sub(h)]
                hop = JUMP if far and k == len(dist) - 1 else 1
                copy_to(src, buf.at[k, :, sub(h)], tr_s.at[f, k, h], tr_r.at[f, k, h], t_dev(sign * hop)).start()

    def t_own():
        rows = t_rows(z)
        total = jnp.zeros((1, SUBW), F32)
        for h in range(NSUB):
            block = tp[rows, sub(h)]
            for sign, dist, buf, f, far in rs_flows:
                last = len(dist) - 1
                here = buf.at[last, :, sub(h)]
                copy_to(here, here, tr_s.at[f, last, h], tr_r.at[f, last, h], right).wait_recv()
                block = block + buf[last, :, sub(h)]
            t_full[rows, sub(h)] = block
            total = total + jnp.sum(block * block, axis=0, keepdims=True)
        return jnp.sum(total)

    def t_ag(s, far_flows):
        k = s - 1
        for h in range(NSUB):
            for sign, dist, buf, f, far in rs_flows:
                n = len(dist)
                if k > n or far != far_flows:
                    continue
                offset = 0 if k == 0 else sign * (k + JUMP - 1 if far else k)
                here = t_full.at[t_rows(z - offset), sub(h)]
                if k:
                    copy_to(here, here, gr_s.at[f, k - 1, h], gr_r.at[f, k - 1, h], right).wait_recv()
                if k < n:
                    hop = JUMP if far and k == 0 else 1
                    copy_to(here, here, gr_s.at[f, k, h], gr_r.at[f, k, h], t_dev(sign * hop)).start()

    def near(s):
        t_ag(s, False)

    def far(s):
        t_ag(s, True)

    loads[2].wait()
    lax.fori_loop(0, 2, t_tile, 0)
    t_rs(1)
    s_half(core)

    for d in order:
        pair_a(d).wait_recv()
        x_to = x_at(d)
        sp[core, :, x_to, 0] = sp[core, :, x_to, 0] + sp_in[:, x_to, 0]
        if d:
            src = sp.at[core, :, x_to, 0]
            copy_to(src, a_in.at[d - 1], one_s.at[0], one_r.at[0], x_peer(d)).start()
        pair_b(d).wait_recv()
        y_to = y_at(d)
        sp[core, y_to, :, 1] = sp[core, y_to, :, 1] + sp_in[y_to, :, 1]
        if d:
            src = sp.at[core, y_to, :, 1]
            copy_to(src, b_in.at[d - 1], one_s.at[1], one_r.at[1], y_peer(d)).start()

    def lt_tile(i, carry):
        at = pl.multiple_of(i * 128, 128)
        lt[pl.ds(at, 128), :] = l_ref[:, pl.ds(at, 128)].astype(F32).T.astype(BF16)
        return carry

    def bt_tile(i, carry):
        at = pl.multiple_of(i * 128, 128)
        index = lax.broadcasted_iota(jnp.int32, (128, NQ), 0) + (at + c * COLS)
        inside = (index >= qc_ref[0:1, :]) & (index < qc_ref[1:2, :])
        bt[pl.ds(at, 128), :] = jnp.where(inside, 1.0, 0.0).astype(BF16)
        return carry

    def answer_tile(i, carry):
        total, norm = carry
        at = pl.multiple_of(i * 256, 256)
        block = v_ref[pl.ds(at, 256), :]
        across = dot(block, bt[...])
        index = lax.broadcasted_iota(jnp.int32, (256, NQ), 0) + (at + z * ROWS)
        inside = (index >= qr_ref[0:1, :]) & (index < qr_ref[1:2, :])
        total = total + jnp.sum(jnp.where(inside, across, 0.0), axis=0, keepdims=True)
        wide = block.astype(F32)
        norm = norm + jnp.sum(wide * wide, axis=0, keepdims=True)
        return total, norm

    def chips_row(base, d):
        return pl.ds(pl.multiple_of(base + lax.rem(yy + NY - d, NY) * 64, 64), 64)

    def forward(full, f, d):
        got = full.at[pl.ds(0, 64 if d else 48)]
        copy_to(got, got, fwd_s.at[f, d], grp_r.at[f, d], other).wait_recv()
        here = full.at[chips_row(keep, d)]
        copy_to(here, here, fwd_s.at[f, d], fwd_r.at[f, d], other).start()

    def forwarded(full, f):
        for d in (0, 1, 3, 2):
            here = full.at[chips_row(give, d)]
            copy_to(here, here, fwd_s.at[f, d], fwd_r.at[f, d], other).wait_recv()

    def x_part(half, first):
        rows = pl.ds(pl.multiple_of(half * 256, 256), 256)

        def tile(i, carry):
            at = pl.multiple_of(i * 256, 256)
            high, low = split(s_full[rows, pl.ds(at, 256)].T)
            have = v_ref[pl.ds(at, 256), :].astype(F32) if first else x1[pl.ds(at, 256), :]
            x1[pl.ds(at, 256), :] = have + dot(high, r_ref[rows, :]) + dot(low, r_ref[rows, :])
            return carry

        lax.fori_loop(0, 4, tile, 0)

    def u_part_of(half):
        rows = pl.ds(pl.multiple_of(half * 256, 256), 256)
        high, low = split(u_full[rows, :].T)
        return dot(high, r_ref[rows, :]) + dot(low, r_ref[rows, :])

    t_rs(2)
    lax.fori_loop(0, 8, lt_tile, 0)
    copy_to(a_in, a_in, one_s.at[0], one_r.at[0], other).wait_recv()
    for d in (2, 1, 3):
        y_to = y_at(d)
        a_sum[d - 1] = sp[core, y_to, xx, 0] + a_in[0, y_to] + a_in[1, y_to] + a_in[2, y_to]
        copy_to(a_sum.at[d - 1], a2_in.at[d - 1], one_s.at[2], one_r.at[2], y_peer(d)).start()
    copy_to(b_in, b_in, one_s.at[1], one_r.at[1], other).wait_recv()
    for d in (2, 1, 3):
        x_to = x_at(d)
        b_sum[d - 1] = sp[core, yy, x_to, 1] + b_in[0, x_to] + b_in[1, x_to] + b_in[2, x_to]
        copy_to(b_sum.at[d - 1], b2_in.at[d - 1], one_s.at[3], one_r.at[3], x_peer(d)).start()
    t_rs(3)
    lax.fori_loop(0, 4, bt_tile, 0)
    own_rows = pl.ds(pl.multiple_of(keep + chip * 16, 16), 16)
    s_a = sp[core, yy, xx, 0] + a_in[0, yy] + a_in[1, yy] + a_in[2, yy]
    s_b = sp[core, yy, xx, 1] + b_in[0, xx] + b_in[1, xx] + b_in[2, xx]
    copy_to(a2_in, a2_in, one_s.at[2], one_r.at[2], other).wait_recv()
    copy_to(b2_in, b2_in, one_s.at[3], one_r.at[3], other).wait_recv()
    s_a = s_a + a2_in[0] + a2_in[1] + a2_in[2]
    s_b = s_b + b2_in[0] + b2_in[1] + b2_in[2]
    s_block = jnp.concatenate([s_a, s_b], axis=0)
    s_full[own_rows, :] = s_block

    def group(j):
        return j // NX

    def s_copy(j):
        here = s_full.at[own_rows]
        return copy_to(here, here, one_s.at[4], grp_r.at[0, group(j)], plane_peer(j))

    def start_all(make):
        def one(j, carry):
            make(j).start()
            return carry

        lax.fori_loop(1, 16, one, 0)

    def start_far(make):
        make(8).start()

        def one(j, carry):
            make(8 - j).start()
            make(8 + j).start()
            return carry

        lax.fori_loop(1, 8, one, 0)

    s_high, s_low = split(s_block)
    u_part = lax.dot_general(s_high, l_ref[...], NT, preferred_element_type=F32) + lax.dot_general(
        s_low, l_ref[...], NT, preferred_element_type=F32
    )
    for i in range(NZ):
        u_out[i] = u_part[i : i + 1, :]

    def u_copy(d):
        return copy_to(u_out.at[lax.rem(z + d, NZ)], u_in.at[d - 1], one_s.at[5], one_r.at[5], z_peer(d))

    start_far(u_copy)
    start_all(s_copy)
    t_rs(4)
    carry = (jnp.zeros((1, NQ), F32), jnp.zeros((1, COLS), F32))
    carry = lax.fori_loop(0, 4, answer_tile, carry)
    copy_to(u_in, u_in, one_s.at[5], one_r.at[5], other).wait_recv()

    def add_row(j, total):
        return total + u_in[j]

    u_row = lax.fori_loop(0, 15, add_row, u_out[z])
    u_all[z] = u_row

    def ug_copy(d):
        return copy_to(u_all.at[z], u_all.at[z], one_s.at[6], one_r.at[6], z_peer(d))

    start_far(ug_copy)
    t_norm = t_own()
    far(1)
    near(1)
    rest = jnp.sum(s_block * s_block) + jnp.sum(u_row * u_row) + t_norm
    lane = lax.broadcasted_iota(jnp.int32, (1, 128), 1)
    for g in range(8):
        m_out[g, :, 0:128] = carry[0][:, g * 128 : g * 128 + 128]
        m_out[g, :, 128:256] = jnp.where(lane < 64, jnp.sum(carry[1]), rest)

    def eighth(d):
        return lax.rem(z + d, 8)

    def m_copy(d):
        return copy_to(m_out.at[eighth(d)], m_z.at[d - 1], one_s.at[7], one_r.at[7], z_peer(d))

    start_far(m_copy)

    near(2)
    far(2)
    for d in (0, 1, 3, 2):
        forward(s_full, 0, d)
    copy_to(u_all.at[0:15], u_all.at[0:15], one_s.at[6], one_r.at[6], other).wait_recv()
    for i in range(NZ):
        u_tile[i : i + 1, :] = u_all[i]
    u_full[own_rows, :] = u_tile[...]

    def up_copy(j):
        here = u_full.at[own_rows]
        return copy_to(here, here, one_s.at[8], grp_r.at[1, group(j)], plane_peer(j))

    start_all(up_copy)
    near(3)
    far(3)
    x_part(core, True)
    copy_to(m_z, m_z, one_s.at[7], one_r.at[7], other).wait_recv()

    def add_m(buffer):
        return lambda j, total: total + buffer[j]

    m_plane[15] = lax.fori_loop(0, 15, add_m(m_z), m_out[eighth(0)])

    def mp_copy(j):
        return copy_to(m_plane.at[15], m_plane.at[j - 1], one_s.at[9], one_r.at[9], plane_peer(j))

    start_all(mp_copy)
    near(4)
    far(4)
    forwarded(s_full, 0)
    x_part(1 - core, False)
    for d in (0, 1, 3, 2):
        forward(u_full, 1, d)
    copy_to(m_plane.at[0:15], m_plane.at[0:15], one_s.at[9], one_r.at[9], other).wait_recv()
    m_pair[0] = lax.fori_loop(0, 16, add_m(m_plane), jnp.zeros((1, 256), F32))
    m_copy_pair = copy_to(m_pair.at[0], m_pair.at[1], one_s.at[12], one_r.at[12], other)
    m_copy_pair.start()
    ur[...] = u_part_of(core)
    forwarded(u_full, 1)
    ur[...] = ur[...] + u_part_of(1 - core)
    near(5)
    far(5)
    m_copy_pair.wait_recv()
    message = m_pair[0] + m_pair[1]
    norm = message[0:1, 128:129]
    alpha = norm / (norm + message[0:1, 192:193])
    high, low = split(t_full[...] + ur[...])
    z_hi[...] = high
    z_lo[...] = low

    def final_tile(i, total):
        at = pl.multiple_of(i * 256, 256)
        rows = lt[pl.ds(at, 256), :]
        image = x1[pl.ds(at, 256), :] + dot(rows, z_hi[...]) + dot(rows, z_lo[...])
        block = v_ref[pl.ds(at, 256), :].astype(F32) - alpha * image
        resid[pl.ds(at, 256), :] = block
        return total + jnp.sum(block * block, axis=0, keepdims=True)

    fresh = lax.fori_loop(0, 4, final_tile, jnp.zeros((1, COLS), F32))
    out_copy = pltpu.make_async_copy(resid, out_ref, out_sem)
    out_copy.start()

    e_z[15, :, 0:128] = jnp.broadcast_to(jnp.sum(fresh), (1, 128))
    e_z[15, :, 128:256] = message[:, 0:128]

    def ez_copy(d):
        return copy_to(e_z.at[15], e_z.at[d - 1], one_s.at[10], one_r.at[10], z_peer(d))

    start_far(ez_copy)
    copy_to(e_z.at[0:15], e_z.at[0:15], one_s.at[10], one_r.at[10], other).wait_recv()
    e_plane[15] = lax.fori_loop(0, 16, add_m(e_z), jnp.zeros((1, 256), F32))

    def ep_copy(j):
        return copy_to(e_plane.at[15], e_plane.at[j - 1], one_s.at[11], one_r.at[11], plane_peer(j))

    start_all(ep_copy)
    spans = (qr_ref[1:2, :] - qr_ref[0:1, :]).astype(F32) * (qc_ref[1:2, :] - qc_ref[0:1, :]).astype(F32)
    scale = alpha / jnp.sqrt(spans)
    for g in range(8):
        slot = lax.rem(z - g - 1 + 2 * NZ, NZ)
        part = slice(g * 128, g * 128 + 128)
        ans_ref[:, part] = e_z[slot, :, 128:256] * scale[:, part]
    copy_to(e_plane.at[0:15], e_plane.at[0:15], one_s.at[11], one_r.at[11], other).wait_recv()
    e_pair[0] = lax.fori_loop(0, 16, add_m(e_plane), jnp.zeros((1, 256), F32))
    e_copy_pair = copy_to(e_pair.at[0], e_pair.at[1], one_s.at[13], one_r.at[13], other)
    e_copy_pair.start()
    e_copy_pair.wait_recv()
    total = e_pair[0] + e_pair[1]
    ratio_ref[...] = total[:, 0:128] / norm

    def sent(ref, sem):
        copy_to(ref, ref, sem, one_r.at[0], other).wait_send()

    for d in range(4):
        sent(sp_in.at[:, 0, 0], pair_s.at[0, d])
        sent(sp_in.at[0, :, 1], pair_s.at[1, d])
        sent(s_full.at[0:64], fwd_s.at[0, d])
        sent(u_full.at[0:64], fwd_s.at[1, d])
    sent(a_in, one_s.at[0])
    sent(b_in, one_s.at[1])
    sent(a2_in, one_s.at[2])
    sent(b2_in, one_s.at[3])
    sent(s_full.at[0:240], one_s.at[4])
    sent(u_in, one_s.at[5])
    sent(u_all.at[0:15], one_s.at[6])
    sent(m_z, one_s.at[7])
    sent(u_full.at[0:240], one_s.at[8])
    sent(m_plane.at[0:15], one_s.at[9])
    sent(e_z.at[0:15], one_s.at[10])
    sent(e_plane.at[0:15], one_s.at[11])
    sent(m_pair.at[0], one_s.at[12])
    sent(e_pair.at[0], one_s.at[13])
    for sign, dist, buf, f, far in rs_flows:
        for k in range(len(dist)):
            for h in range(NSUB):
                sent(buf.at[k, :, sub(h)], tr_s.at[f, k, h])
                sent(buf.at[k, :, sub(h)], gr_s.at[f, k, h])
    out_copy.wait()


def shards(right_side, theta_left, theta_right, query_rows, query_cols):
    vmem = pl.BlockSpec(memory_space=pltpu.VMEM)
    hbm = pl.BlockSpec(memory_space=pltpu.HBM)
    dma = pltpu.SemaphoreType.DMA
    residual, answers, ratio = pl.pallas_call(
        kernel,
        out_shape=(
            jax.ShapeDtypeStruct((ROWS, COLS), F32),
            jax.ShapeDtypeStruct((1, NQ), F32),
            jax.ShapeDtypeStruct((1, 128), F32),
        ),
        in_specs=[hbm] * 3 + [vmem] * 2,
        out_specs=(hbm, vmem, vmem),
        scratch_shapes=[
            pltpu.VMEM((ROWS, COLS), BF16),
            pltpu.VMEM((Q, ROWS), BF16),
            pltpu.VMEM((Q, COLS), BF16),
            pltpu.VMEM((ROWS, Q), BF16),
            pltpu.VMEM((COLS, NQ), BF16),
            pltpu.VMEM((2, NY, NX, 2, 8, ROWS), F32),
            pltpu.VMEM((NY, NX, 2, 8, ROWS), F32),
            pltpu.VMEM((3, NY, 8, ROWS), F32),
            pltpu.VMEM((3, NX, 8, ROWS), F32),
            pltpu.VMEM((3, 8, ROWS), F32),
            pltpu.VMEM((3, 8, ROWS), F32),
            pltpu.VMEM((3, 8, ROWS), F32),
            pltpu.VMEM((3, 8, ROWS), F32),
            pltpu.VMEM((Q, ROWS), F32),
            pltpu.VMEM((Q, COLS), F32),
            pltpu.VMEM((JUMP - 1, 32, COLS), F32),
            pltpu.VMEM((JUMP - 1, 32, COLS), F32),
            pltpu.VMEM((8 - JUMP, 32, COLS), F32),
            pltpu.VMEM((9 - JUMP, 32, COLS), F32),
            pltpu.VMEM((Q, COLS), F32),
            pltpu.VMEM((NZ, 1, Q), F32),
            pltpu.VMEM((15, 1, Q), F32),
            pltpu.VMEM((NZ, 1, Q), F32),
            pltpu.VMEM((NZ, Q), F32),
            pltpu.VMEM((Q, Q), F32),
            pltpu.VMEM((Q, COLS), F32),
            pltpu.VMEM((ROWS, COLS), F32),
            pltpu.VMEM((ROWS, COLS), F32),
            pltpu.VMEM((Q, COLS), BF16),
            pltpu.VMEM((Q, COLS), BF16),
            pltpu.VMEM((8, 1, 256), F32),
            pltpu.VMEM((15, 1, 256), F32),
            pltpu.VMEM((16, 1, 256), F32),
            pltpu.VMEM((2, 1, 256), F32),
            pltpu.VMEM((16, 1, 256), F32),
            pltpu.VMEM((16, 1, 256), F32),
            pltpu.VMEM((2, 1, 256), F32),
            dma((2, 4)), dma((2, 4)),
            dma((14,)), dma((14,)),
            dma((2, 4)),
            dma((2, 4)), dma((2, 4)),
            dma((4, 8, NSUB)), dma((4, 8, NSUB)),
            dma((4, 8, NSUB)), dma((4, 8, NSUB)),
            dma((3,)),
            dma,
        ],
        compiler_params=pltpu.CompilerParams(
            collective_id=0, has_side_effects=True, vmem_limit_bytes=60 * 1024 * 1024
        ),
        name="step",
    )(right_side, theta_left, theta_right, query_rows.T, query_cols.T)
    return residual, ratio[0, 0:1], answers.reshape(NQ)


def solution(mesh):
    return jax.shard_map(
        shards,
        mesh=mesh,
        in_specs=(P("row", "col"), P(None, "row"), P(None, "col"), P(), P()),
        out_specs=(P("row", "col"), P(), P()),
        check_vma=False,
    )
```

```python
import functools

import jax
import jax.numpy as jnp
from jax import lax
from jax.experimental import pallas as pl
from jax.experimental.pallas import tpu as pltpu
from jax.sharding import PartitionSpec as P

MESH = pl.DeviceIdType.MESH
F32, BF16 = jnp.float32, jnp.bfloat16
NZ, NX, NY = 16, 4, 4
ROWS, COLS, Q, NQ = 1024, 512, 512, 1024
NSUB = 1
JUMP = 5
GATHER = 5
SUBW = COLS // NSUB
NT = (((1,), (1,)), ((), ()))


def dot(a, b):
    return jnp.dot(a, b, preferred_element_type=F32)


def split(value):
    high = value.astype(BF16)
    return high, (value - high.astype(F32)).astype(BF16)


def dot_split(value, b):
    high, low = split(value)
    return dot(high, b) + dot(low, b)


def copy_to(src, dst, send, recv, device):
    return pltpu.make_async_remote_copy(
        src_ref=src, dst_ref=dst, send_sem=send, recv_sem=recv, device_id=device, device_id_type=MESH
    )


def kernel(
    v_hbm, l_hbm, r_hbm, qr_ref, qc_ref,
    out_ref, ans_ref, ratio_ref,
    v_ref, l_ref, r_ref,
    lt, bt, sp, sp_in, a_in, b_in, a_sum, b_sum, a2_in, b2_in, s_full,
    tp, t_near_r, t_near_l, t_far_r, t_far_l, t_full, u_out, u_in, u_all, u_tile, u_full, ur,
    x1, resid, z_hi, z_lo, m_out, m_z, m_plane, m_pair, e_z, e_plane, e_pair,
    pair_s, pair_r, one_s, one_r, grp_r, fwd_s, fwd_r, tr_s, tr_r, gr_s, gr_r, in_sem, out_sem,
):
    z = lax.axis_index("row")
    c = lax.axis_index("col")
    core = lax.rem(c, 2)
    chip = c // 2
    xx = lax.rem(chip, NX)
    yy = chip // NX

    def z_peer(d):
        return (lax.rem(z + d, NZ), c)

    def plane_chip(j):
        return lax.rem(yy + j // NX, NY) * NX + lax.rem(xx + lax.rem(j, NX), NX)

    def plane_peer(j):
        return (z, plane_chip(j) * 2 + core)

    def x_peer(d):
        return (z, (yy * NX + lax.rem(xx + d, NX)) * 2 + core)

    def y_peer(d):
        return (z, (lax.rem(yy + d, NY) * NX + xx) * 2 + core)

    other = (z, chip * 2 + 1 - core)
    right, left = z_peer(1), z_peer(NZ - 1)

    loads = [
        pltpu.make_async_copy(src, dst, in_sem.at[i])
        for i, (src, dst) in enumerate(((r_hbm, r_ref), (v_hbm, v_ref), (l_hbm, l_ref)))
    ]
    for load in loads:
        load.start()
    barrier = pltpu.get_barrier_semaphore()

    def greet(d, carry):
        pl.semaphore_signal(barrier, inc=1, device_id=z_peer(d), device_id_type=MESH)
        pl.semaphore_signal(barrier, inc=1, device_id=plane_peer(d), device_id_type=MESH)
        return carry

    pl.semaphore_signal(barrier, inc=1, device_id=other, device_id_type=MESH)
    lax.fori_loop(1, NZ, greet, 0)

    def s_half(half):
        rows = pl.ds(pl.multiple_of(half * 256, 256), 256)

        def tile(i, carry):
            at = pl.multiple_of(i * 256, 256)
            block = lax.dot_general(r_ref[rows, :], v_ref[pl.ds(at, 256), :], NT, preferred_element_type=F32)
            sp[half, :, :, :, :, pl.ds(at, 256)] = block.reshape(NY, NX, 2, 8, 256)
            return carry

        lax.fori_loop(0, 4, tile, 0)

    def t_tile(i, carry):
        at = pl.multiple_of(i * 256, 256)
        tp[pl.ds(at, 256), :] = dot(l_ref[pl.ds(at, 256), :], v_ref[...])
        return carry

    loads[0].wait()
    loads[1].wait()
    s_half(1 - core)
    pl.semaphore_wait(barrier, 31)

    give, keep = (1 - core) * 256, core * 256
    order = (2, 1, 3, 0)

    def x_at(d):
        return lax.rem(xx + d, NX)

    def y_at(d):
        return lax.rem(yy + d, NY)

    def pair_a(d):
        return copy_to(
            sp.at[1 - core, :, x_at(d), 0], sp_in.at[:, x_at(d), 0], pair_s.at[0, d], pair_r.at[0, d], other
        )

    def pair_b(d):
        return copy_to(
            sp.at[1 - core, y_at(d), :, 1], sp_in.at[y_at(d), :, 1], pair_s.at[1, d], pair_r.at[1, d], other
        )

    for d in order:
        pair_a(d).start()
        pair_b(d).start()

    def t_rows(block):
        return pl.ds(pl.multiple_of(lax.rem(block + 2 * NZ, NZ) * 32, 32), 32)

    def sub(h):
        return pl.ds(h * SUBW, SUBW)

    rs_flows = (
        (1, tuple(range(7, JUMP - 1, -1)), t_far_r, 2, True),
        (-1, tuple(range(8, JUMP - 1, -1)), t_far_l, 3, True),
        (1, tuple(range(JUMP - 1, 0, -1)), t_near_r, 0, False),
        (-1, tuple(range(JUMP - 1, 0, -1)), t_near_l, 1, False),
    )

    def t_dev(offset):
        return z_peer(offset + NZ)

    def t_rs(s):
        k = s - 1
        for h in range(NSUB):
            for sign, dist, buf, f, far in rs_flows:
                if k >= len(dist):
                    continue
                rows = t_rows(z + sign * dist[k])
                src = tp.at[rows, sub(h)]
                if k:
                    src = buf.at[k - 1, :, sub(h)]
                    copy_to(src, src, tr_s.at[f, k - 1, h], tr_r.at[f, k - 1, h], right).wait_recv()
                    buf[k - 1, :, sub(h)] = buf[k - 1, :, sub(h)] + tp[rows, sub(h)]
                hop = JUMP if far and k == len(dist) - 1 else 1
                copy_to(src, buf.at[k, :, sub(h)], tr_s.at[f, k, h], tr_r.at[f, k, h], t_dev(sign * hop)).start()

    def t_own():
        rows = t_rows(z)
        total = jnp.zeros((1, SUBW), F32)
        for h in range(NSUB):
            block = tp[rows, sub(h)]
            for sign, dist, buf, f, far in rs_flows:
                last = len(dist) - 1
                here = buf.at[last, :, sub(h)]
                copy_to(here, here, tr_s.at[f, last, h], tr_r.at[f, last, h], right).wait_recv()
                block = block + buf[last, :, sub(h)]
            t_full[rows, sub(h)] = block
            total = total + jnp.sum(block * block, axis=0, keepdims=True)
        return jnp.sum(total)

    def ag_count(sign, far):
        return (8 if sign > 0 else 9) - GATHER if far else GATHER - 1

    def t_ag(s, far_flows):
        k = s - 1
        for h in range(NSUB):
            for sign, dist, buf, f, far in rs_flows:
                n = ag_count(sign, far)
                if k > n or far != far_flows:
                    continue
                offset = 0 if k == 0 else sign * (k + GATHER - 1 if far else k)
                here = t_full.at[t_rows(z - offset), sub(h)]
                if k:
                    copy_to(here, here, gr_s.at[f, k - 1, h], gr_r.at[f, k - 1, h], right).wait_recv()
                if k < n:
                    hop = GATHER if far and k == 0 else 1
                    copy_to(here, here, gr_s.at[f, k, h], gr_r.at[f, k, h], t_dev(sign * hop)).start()

    def near(s):
        t_ag(s, False)

    def far(s):
        t_ag(s, True)

    loads[2].wait()
    lax.fori_loop(0, 2, t_tile, 0)
    t_rs(1)
    s_half(core)

    for d in order:
        pair_a(d).wait_recv()
        x_to = x_at(d)
        sp[core, :, x_to, 0] = sp[core, :, x_to, 0] + sp_in[:, x_to, 0]
        if d:
            src = sp.at[core, :, x_to, 0]
            copy_to(src, a_in.at[d - 1], one_s.at[0], one_r.at[0], x_peer(d)).start()
        pair_b(d).wait_recv()
        y_to = y_at(d)
        sp[core, y_to, :, 1] = sp[core, y_to, :, 1] + sp_in[y_to, :, 1]
        if d:
            src = sp.at[core, y_to, :, 1]
            copy_to(src, b_in.at[d - 1], one_s.at[1], one_r.at[1], y_peer(d)).start()

    def lt_tile(i, carry):
        at = pl.multiple_of(i * 128, 128)
        lt[pl.ds(at, 128), :] = l_ref[:, pl.ds(at, 128)].astype(F32).T.astype(BF16)
        return carry

    def bt_tile(i, carry):
        at = pl.multiple_of(i * 128, 128)
        index = lax.broadcasted_iota(jnp.int32, (128, NQ), 0) + (at + c * COLS)
        inside = (index >= qc_ref[0:1, :]) & (index < qc_ref[1:2, :])
        bt[pl.ds(at, 128), :] = jnp.where(inside, 1.0, 0.0).astype(BF16)
        return carry

    def answer_tile(i, carry):
        total, norm = carry
        at = pl.multiple_of(i * 256, 256)
        block = v_ref[pl.ds(at, 256), :]
        across = dot(block, bt[...])
        index = lax.broadcasted_iota(jnp.int32, (256, NQ), 0) + (at + z * ROWS)
        inside = (index >= qr_ref[0:1, :]) & (index < qr_ref[1:2, :])
        total = total + jnp.sum(jnp.where(inside, across, 0.0), axis=0, keepdims=True)
        wide = block.astype(F32)
        norm = norm + jnp.sum(wide * wide, axis=0, keepdims=True)
        return total, norm

    def chips_row(base, d):
        return pl.ds(pl.multiple_of(base + lax.rem(yy + NY - d, NY) * 64, 64), 64)

    def forward(full, f, d):
        got = full.at[pl.ds(0, 64 if d else 48)]
        copy_to(got, got, fwd_s.at[f, d], grp_r.at[f, d], other).wait_recv()
        here = full.at[chips_row(keep, d)]
        copy_to(here, here, fwd_s.at[f, d], fwd_r.at[f, d], other).start()

    def forwarded(full, f):
        for d in (0, 1, 3, 2):
            here = full.at[chips_row(give, d)]
            copy_to(here, here, fwd_s.at[f, d], fwd_r.at[f, d], other).wait_recv()

    def x_part(half, first):
        rows = pl.ds(pl.multiple_of(half * 256, 256), 256)

        def tile(i, carry):
            at = pl.multiple_of(i * 256, 256)
            high, low = split(s_full[rows, pl.ds(at, 256)].T)
            have = v_ref[pl.ds(at, 256), :].astype(F32) if first else x1[pl.ds(at, 256), :]
            x1[pl.ds(at, 256), :] = have + dot(high, r_ref[rows, :]) + dot(low, r_ref[rows, :])
            return carry

        lax.fori_loop(0, 4, tile, 0)

    def u_part_of(half):
        rows = pl.ds(pl.multiple_of(half * 256, 256), 256)
        high, low = split(u_full[rows, :].T)
        return dot(high, r_ref[rows, :]) + dot(low, r_ref[rows, :])

    t_rs(2)
    lax.fori_loop(0, 8, lt_tile, 0)
    copy_to(a_in, a_in, one_s.at[0], one_r.at[0], other).wait_recv()
    for d in (2, 1, 3):
        y_to = y_at(d)
        a_sum[d - 1] = sp[core, y_to, xx, 0] + a_in[0, y_to] + a_in[1, y_to] + a_in[2, y_to]
        copy_to(a_sum.at[d - 1], a2_in.at[d - 1], one_s.at[2], one_r.at[2], y_peer(d)).start()
    copy_to(b_in, b_in, one_s.at[1], one_r.at[1], other).wait_recv()
    for d in (2, 1, 3):
        x_to = x_at(d)
        b_sum[d - 1] = sp[core, yy, x_to, 1] + b_in[0, x_to] + b_in[1, x_to] + b_in[2, x_to]
        copy_to(b_sum.at[d - 1], b2_in.at[d - 1], one_s.at[3], one_r.at[3], x_peer(d)).start()
    t_rs(3)
    own_rows = pl.ds(pl.multiple_of(keep + chip * 16, 16), 16)
    s_a = sp[core, yy, xx, 0] + a_in[0, yy] + a_in[1, yy] + a_in[2, yy]
    s_b = sp[core, yy, xx, 1] + b_in[0, xx] + b_in[1, xx] + b_in[2, xx]
    copy_to(a2_in, a2_in, one_s.at[2], one_r.at[2], other).wait_recv()
    copy_to(b2_in, b2_in, one_s.at[3], one_r.at[3], other).wait_recv()
    s_a = s_a + a2_in[0] + a2_in[1] + a2_in[2]
    s_b = s_b + b2_in[0] + b2_in[1] + b2_in[2]
    s_block = jnp.concatenate([s_a, s_b], axis=0)
    s_full[own_rows, :] = s_block

    def group(j):
        return j // NX

    def s_copy(j):
        here = s_full.at[own_rows]
        return copy_to(here, here, one_s.at[4], grp_r.at[0, group(j)], plane_peer(j))

    def start_all(make):
        def one(j, carry):
            make(j).start()
            return carry

        lax.fori_loop(1, 16, one, 0)

    def start_far(make):
        make(8).start()

        def one(j, carry):
            make(8 - j).start()
            make(8 + j).start()
            return carry

        lax.fori_loop(1, 8, one, 0)

    s_high, s_low = split(s_block)
    u_part = lax.dot_general(s_high, l_ref[...], NT, preferred_element_type=F32) + lax.dot_general(
        s_low, l_ref[...], NT, preferred_element_type=F32
    )
    for i in range(NZ):
        u_out[i] = u_part[i : i + 1, :]

    def u_copy(d):
        return copy_to(u_out.at[lax.rem(z + d, NZ)], u_in.at[d - 1], one_s.at[5], one_r.at[5], z_peer(d))

    start_far(u_copy)
    start_all(s_copy)
    t_rs(4)
    copy_to(u_in, u_in, one_s.at[5], one_r.at[5], other).wait_recv()

    def add_row(j, total):
        return total + u_in[j]

    u_row = lax.fori_loop(0, 15, add_row, u_out[z])
    u_all[z] = u_row

    def ug_copy(d):
        return copy_to(u_all.at[z], u_all.at[z], one_s.at[6], one_r.at[6], z_peer(d))

    start_far(ug_copy)
    t_norm = t_own()
    far(1)
    near(1)
    lax.fori_loop(0, 4, bt_tile, 0)
    carry = (jnp.zeros((1, NQ), F32), jnp.zeros((1, COLS), F32))
    carry = lax.fori_loop(0, 4, answer_tile, carry)
    rest = jnp.sum(s_block * s_block) + jnp.sum(u_row * u_row) + t_norm
    lane = lax.broadcasted_iota(jnp.int32, (1, 128), 1)
    for g in range(8):
        m_out[g, :, 0:128] = carry[0][:, g * 128 : g * 128 + 128]
        m_out[g, :, 128:256] = jnp.where(lane < 64, jnp.sum(carry[1]), rest)

    def eighth(d):
        return lax.rem(z + d, 8)

    def m_copy(d):
        return copy_to(m_out.at[eighth(d)], m_z.at[d - 1], one_s.at[7], one_r.at[7], z_peer(d))

    start_far(m_copy)

    near(2)
    copy_to(u_all.at[0:15], u_all.at[0:15], one_s.at[6], one_r.at[6], other).wait_recv()
    for i in range(NZ):
        u_tile[i : i + 1, :] = u_all[i]
    u_full[own_rows, :] = u_tile[...]

    def up_copy(j):
        here = u_full.at[own_rows]
        return copy_to(here, here, one_s.at[8], grp_r.at[1, group(j)], plane_peer(j))

    start_all(up_copy)
    far(2)
    near(3)
    far(3)
    for d in (0, 1, 3, 2):
        forward(s_full, 0, d)
    x_part(core, True)
    copy_to(m_z, m_z, one_s.at[7], one_r.at[7], other).wait_recv()

    def add_m(buffer):
        return lambda j, total: total + buffer[j]

    m_plane[15] = lax.fori_loop(0, 15, add_m(m_z), m_out[eighth(0)])

    def mp_copy(j):
        return copy_to(m_plane.at[15], m_plane.at[j - 1], one_s.at[9], one_r.at[9], plane_peer(j))

    start_all(mp_copy)
    near(4)
    far(4)
    forwarded(s_full, 0)
    x_part(1 - core, False)
    for d in (0, 1, 3, 2):
        forward(u_full, 1, d)
    copy_to(m_plane.at[0:15], m_plane.at[0:15], one_s.at[9], one_r.at[9], other).wait_recv()
    m_pair[0] = lax.fori_loop(0, 16, add_m(m_plane), jnp.zeros((1, 256), F32))
    m_copy_pair = copy_to(m_pair.at[0], m_pair.at[1], one_s.at[12], one_r.at[12], other)
    m_copy_pair.start()
    ur[...] = u_part_of(core)
    forwarded(u_full, 1)
    ur[...] = ur[...] + u_part_of(1 - core)
    near(5)
    far(5)
    m_copy_pair.wait_recv()
    message = m_pair[0] + m_pair[1]
    norm = message[0:1, 128:129]
    alpha = norm / (norm + message[0:1, 192:193])
    high, low = split(t_full[...] + ur[...])
    z_hi[...] = high
    z_lo[...] = low

    def final_tile(i, total):
        at = pl.multiple_of(i * 256, 256)
        rows = lt[pl.ds(at, 256), :]
        image = x1[pl.ds(at, 256), :] + dot(rows, z_hi[...]) + dot(rows, z_lo[...])
        block = v_ref[pl.ds(at, 256), :].astype(F32) - alpha * image
        resid[pl.ds(at, 256), :] = block
        return total + jnp.sum(block * block, axis=0, keepdims=True)

    fresh = lax.fori_loop(0, 4, final_tile, jnp.zeros((1, COLS), F32))
    out_copy = pltpu.make_async_copy(resid, out_ref, out_sem)
    out_copy.start()

    e_z[15, :, 0:128] = jnp.broadcast_to(jnp.sum(fresh), (1, 128))
    e_z[15, :, 128:256] = message[:, 0:128]

    def ez_copy(d):
        return copy_to(e_z.at[15], e_z.at[d - 1], one_s.at[10], one_r.at[10], z_peer(d))

    start_far(ez_copy)
    copy_to(e_z.at[0:15], e_z.at[0:15], one_s.at[10], one_r.at[10], other).wait_recv()
    e_plane[15] = lax.fori_loop(0, 16, add_m(e_z), jnp.zeros((1, 256), F32))

    def ep_copy(j):
        return copy_to(e_plane.at[15], e_plane.at[j - 1], one_s.at[11], one_r.at[11], plane_peer(j))

    start_all(ep_copy)
    spans = (qr_ref[1:2, :] - qr_ref[0:1, :]).astype(F32) * (qc_ref[1:2, :] - qc_ref[0:1, :]).astype(F32)
    scale = alpha / jnp.sqrt(spans)
    for g in range(8):
        slot = lax.rem(z - g - 1 + 2 * NZ, NZ)
        part = slice(g * 128, g * 128 + 128)
        ans_ref[:, part] = e_z[slot, :, 128:256] * scale[:, part]
    copy_to(e_plane.at[0:15], e_plane.at[0:15], one_s.at[11], one_r.at[11], other).wait_recv()
    e_pair[0] = lax.fori_loop(0, 16, add_m(e_plane), jnp.zeros((1, 256), F32))
    e_copy_pair = copy_to(e_pair.at[0], e_pair.at[1], one_s.at[13], one_r.at[13], other)
    e_copy_pair.start()
    e_copy_pair.wait_recv()
    total = e_pair[0] + e_pair[1]
    ratio_ref[...] = total[:, 0:128] / norm

    def sent(ref, sem):
        copy_to(ref, ref, sem, one_r.at[0], other).wait_send()

    for d in range(4):
        sent(sp_in.at[:, 0, 0], pair_s.at[0, d])
        sent(sp_in.at[0, :, 1], pair_s.at[1, d])
        sent(s_full.at[0:64], fwd_s.at[0, d])
        sent(u_full.at[0:64], fwd_s.at[1, d])
    sent(a_in, one_s.at[0])
    sent(b_in, one_s.at[1])
    sent(a2_in, one_s.at[2])
    sent(b2_in, one_s.at[3])
    sent(s_full.at[0:240], one_s.at[4])
    sent(u_in, one_s.at[5])
    sent(u_all.at[0:15], one_s.at[6])
    sent(m_z, one_s.at[7])
    sent(u_full.at[0:240], one_s.at[8])
    sent(m_plane.at[0:15], one_s.at[9])
    sent(e_z.at[0:15], one_s.at[10])
    sent(e_plane.at[0:15], one_s.at[11])
    sent(m_pair.at[0], one_s.at[12])
    sent(e_pair.at[0], one_s.at[13])
    for sign, dist, buf, f, far in rs_flows:
        for k in range(ag_count(sign, far)):
            for h in range(NSUB):
                sent(buf.at[0, :, sub(h)], gr_s.at[f, k, h])
        for k in range(len(dist)):
            for h in range(NSUB):
                sent(buf.at[k, :, sub(h)], tr_s.at[f, k, h])
    out_copy.wait()


def shards(right_side, theta_left, theta_right, query_rows, query_cols):
    vmem = pl.BlockSpec(memory_space=pltpu.VMEM)
    hbm = pl.BlockSpec(memory_space=pltpu.HBM)
    dma = pltpu.SemaphoreType.DMA
    residual, answers, ratio = pl.pallas_call(
        kernel,
        out_shape=(
            jax.ShapeDtypeStruct((ROWS, COLS), F32),
            jax.ShapeDtypeStruct((1, NQ), F32),
            jax.ShapeDtypeStruct((1, 128), F32),
        ),
        in_specs=[hbm] * 3 + [vmem] * 2,
        out_specs=(hbm, vmem, vmem),
        scratch_shapes=[
            pltpu.VMEM((ROWS, COLS), BF16),
            pltpu.VMEM((Q, ROWS), BF16),
            pltpu.VMEM((Q, COLS), BF16),
            pltpu.VMEM((ROWS, Q), BF16),
            pltpu.VMEM((COLS, NQ), BF16),
            pltpu.VMEM((2, NY, NX, 2, 8, ROWS), F32),
            pltpu.VMEM((NY, NX, 2, 8, ROWS), F32),
            pltpu.VMEM((3, NY, 8, ROWS), F32),
            pltpu.VMEM((3, NX, 8, ROWS), F32),
            pltpu.VMEM((3, 8, ROWS), F32),
            pltpu.VMEM((3, 8, ROWS), F32),
            pltpu.VMEM((3, 8, ROWS), F32),
            pltpu.VMEM((3, 8, ROWS), F32),
            pltpu.VMEM((Q, ROWS), F32),
            pltpu.VMEM((Q, COLS), F32),
            pltpu.VMEM((JUMP - 1, 32, COLS), F32),
            pltpu.VMEM((JUMP - 1, 32, COLS), F32),
            pltpu.VMEM((8 - JUMP, 32, COLS), F32),
            pltpu.VMEM((9 - JUMP, 32, COLS), F32),
            pltpu.VMEM((Q, COLS), F32),
            pltpu.VMEM((NZ, 1, Q), F32),
            pltpu.VMEM((15, 1, Q), F32),
            pltpu.VMEM((NZ, 1, Q), F32),
            pltpu.VMEM((NZ, Q), F32),
            pltpu.VMEM((Q, Q), F32),
            pltpu.VMEM((Q, COLS), F32),
            pltpu.VMEM((ROWS, COLS), F32),
            pltpu.VMEM((ROWS, COLS), F32),
            pltpu.VMEM((Q, COLS), BF16),
            pltpu.VMEM((Q, COLS), BF16),
            pltpu.VMEM((8, 1, 256), F32),
            pltpu.VMEM((15, 1, 256), F32),
            pltpu.VMEM((16, 1, 256), F32),
            pltpu.VMEM((2, 1, 256), F32),
            pltpu.VMEM((16, 1, 256), F32),
            pltpu.VMEM((16, 1, 256), F32),
            pltpu.VMEM((2, 1, 256), F32),
            dma((2, 4)), dma((2, 4)),
            dma((14,)), dma((14,)),
            dma((2, 4)),
            dma((2, 4)), dma((2, 4)),
            dma((4, 8, NSUB)), dma((4, 8, NSUB)),
            dma((4, 8, NSUB)), dma((4, 8, NSUB)),
            dma((3,)),
            dma,
        ],
        compiler_params=pltpu.CompilerParams(
            collective_id=0, has_side_effects=True, vmem_limit_bytes=60 * 1024 * 1024
        ),
        name="step",
    )(right_side, theta_left, theta_right, query_rows.T, query_cols.T)
    return residual, ratio[0, 0:1], answers.reshape(NQ)


def solution(mesh):
    return jax.shard_map(
        shards,
        mesh=mesh,
        in_specs=(P("row", "col"), P(None, "row"), P(None, "col"), P(), P()),
        out_specs=(P("row", "col"), P(), P()),
        check_vma=False,
    )
```
